32 devices in a mesh: lon: 8 (over z, y), lat: 4 (over x, core).
Axes of the slice: x: 2, y: 2, z: 4, core: 2. Of those that a mesh axis runs over, the one named last changes fastest.
Arguments:
- latent_state: bfloat16 [128, 64, 512], P('lon', 'lat'), may hold values from -6 to 6
- cotangent: bfloat16 [128, 64, 512], P('lon', 'lat'), may hold values from -6 to 6
- w_inner: bfloat16 [512, 1024], replicated, may hold values from -0.25 to 0.25
- w_outer: bfloat16 [1024, 512], replicated, may hold values from -0.1875 to 0.1875
- norm_gain: float32 [512], replicated, may hold values from 0.5 to 1.5
- source_block: int32 [128, 64], P('lon', 'lat'), may hold values from 0 to 31, as said below
- corner_code: int32 [128, 64], P('lon', 'lat'), may hold values from 0 to 54, as said below
- frac_lon: float32 [128, 64], P('lon', 'lat'), may hold values from 0 to 1
- frac_lat: float32 [128, 64], P('lon', 'lat'), may hold values from 0 to 1
- terrain: int32 [128, 64], P('lon', 'lat'), may hold values from 0 to 7
- kappa_table: float32 [8], replicated, may hold values from 0.05 to 0.24
Outputs:
- state_out: bfloat16 [128, 64, 512], P('lon', 'lat')
- state_grad: bfloat16 [128, 64, 512], P('lon', 'lat')
- grad_inner: float32 [512, 1024], replicated
- grad_outer: float32 [1024, 512], replicated
- grad_gain: float32 [512], replicated
The draws below stay inside these ranges and needn't reach their ends.
Inputs may be any that keep to these rules, and one draw needn't show every extreme that they name: `source_block`: the block's latitude part lies in the target's own lat tile; values run over all 8 x 8 blocks of that tile row. Row corner_code // 8 and column corner_code % 8 are both at most 6.
All inputs are finite; a program needn't handle non-finite values.
Results may differ from the reference program's by a relative error of at most 0.017.
Values may be sent and summed in bfloat16 or wider, within the bound.
No kernel may reach another device: no remote copies, remote signals or barrier semaphores. Data moves between devices by JAX's collectives and lax.ppermute only.
A program may use at most 128 MiB of HBM per device.

```python
import jax
import jax.numpy as jnp
from jax import lax

C = 512
HID = 1024
STEPS = 4
NCLASS = 8
TLAT = 16
NLON = 128
NLAT = 64


def draw_source_block(key, part):
    blocks = NLON // 8
    tiles = NLAT // TLAT
    per_row = TLAT // 8
    lon_cell = jnp.arange(NLON, dtype=jnp.int32)[:, None]
    lat_cell = jnp.arange(NLAT, dtype=jnp.int32)[None, :]
    distance = jnp.abs(2 * (lat_cell // TLAT) + 1 - tiles)
    reach = 1 + (blocks // 2 - 1) * distance // max(tiles - 1, 1)
    reach = jnp.broadcast_to(reach, (NLON, NLAT))
    first_key = jax.random.fold_in(key, 11)
    second_key = jax.random.fold_in(key, 12)
    third_key = jax.random.fold_in(key, 13)
    fourth_key = jax.random.fold_in(key, 14)
    offset = jax.random.randint(first_key, (NLON, NLAT), -reach, reach + 1)
    far_pick = jax.random.randint(third_key, (NLON, NLAT), 0, 4) == 0
    far_offset = jax.random.randint(fourth_key, (NLON, NLAT), -(blocks // 2), blocks // 2 + 1)
    offset = jnp.where(far_pick, far_offset, offset)
    polar = jnp.broadcast_to(distance == tiles - 1, (NLON, NLAT))
    marked = jnp.logical_and(lon_cell % 8 == 0, lat_cell % TLAT == 0)
    offset = jnp.where(jnp.logical_and(polar, marked), blocks // 2, offset)
    lon_block = (lon_cell // 8 + offset) % blocks
    lat_block = jax.random.randint(second_key, (NLON, NLAT), 0, per_row)
    return (lon_block * per_row + lat_block).astype(jnp.int32)


def draw_corner_code(key, part):
    first_key = jax.random.fold_in(key, 21)
    second_key = jax.random.fold_in(key, 22)
    row_part = jax.random.randint(first_key, (NLON, NLAT), 0, 7)
    col_part = jax.random.randint(second_key, (NLON, NLAT), 0, 7)
    return (row_part * 8 + col_part).astype(jnp.int32)


def place_ends(result, own_key, low, top_value):
    longest = result.shape.index(max(result.shape))
    spots = []
    for shift in (0, 1):
        where = [jax.random.randint(jax.random.fold_in(own_key, axis), (), 0, length) for axis, length in enumerate(result.shape)]
        where[longest] = (where[longest] + shift) % result.shape[longest]
        spots.append(tuple(where))
    return result.at[spots[0]].set(low).at[spots[1]].set(top_value)


def block_scale(stream_key, shape, cuts, low, high):
    level = 1.0
    for axis_at, blocks in cuts:
        heights = jax.random.uniform(jax.random.fold_in(jax.random.fold_in(stream_key, 6), axis_at), (blocks,), jnp.float32, low / len(cuts), high / len(cuts))
        level = level * jnp.repeat(jnp.exp(heights), shape[axis_at] // blocks).reshape((-1,) + (1,) * (len(shape) - 1 - axis_at))
    return level


def centred(own_key, dims, scale, most, cuts=(), held_as=jnp.bfloat16):
    array = jax.random.normal(own_key, dims, jnp.float32) * scale
    if len(cuts) > 0:
        array = block_scale(own_key, dims, cuts, -0.22, 0.18) * array
    return jnp.clip(array, min=-most, max=most).astype(held_as)


def setup_inputs(seed: int = 0) -> dict:
    key_list = jax.random.split(jax.random.key(seed), 12)
    return {
        "latent_state": centred(key_list[0], (NLON, NLAT, C), 1.0, 6.0, ((0, 8), (1, 4))),
        "cotangent": centred(key_list[1], (NLON, NLAT, C), 1.0, 6.0, ((0, 8), (1, 4))),
        "w_inner": centred(key_list[2], (C, HID), C ** -0.5, 0.25),
        "w_outer": centred(key_list[3], (HID, C), HID ** -0.5, 0.1875),
        "norm_gain": jnp.clip(1.0 + 0.1 * jax.random.normal(key_list[4], (C,), jnp.float32), 0.5, 1.5),
        "source_block": draw_source_block(jax.random.fold_in(key_list[11], 71), 0),
        "corner_code": draw_corner_code(jax.random.fold_in(key_list[11], 71), 0),
        "frac_lon": jnp.clip(1.0 * jax.random.uniform(key_list[7], (NLON, NLAT), jnp.float32) ** block_scale(key_list[7], (NLON, NLAT), ((0, 8), (1, 4)), -0.2, 0.2), 0.0, 1.0),
        "frac_lat": jnp.clip(1.0 * jax.random.uniform(key_list[8], (NLON, NLAT), jnp.float32) ** block_scale(key_list[8], (NLON, NLAT), ((0, 8), (1, 4)), -0.2, 0.2), 0.0, 1.0),
        "terrain": place_ends(jax.random.randint(key_list[9], (NLON, NLAT), 0, NCLASS), jax.random.fold_in(key_list[9], 1), 0, NCLASS - 1).astype(jnp.int32),
        "kappa_table": jnp.clip(jax.random.uniform(key_list[10], (NCLASS,), jnp.float32, 0.05, 0.24), 0.05, 0.24),
    }


def source_cells(source_block, corner_code):
    per_row = TLAT // 8
    lat_tile = (jnp.arange(NLAT, dtype=jnp.int32) // TLAT)[None, :]
    lon_source = source_block // per_row * 8 + corner_code // 8
    lat_source = lat_tile * TLAT + source_block % per_row * 8 + corner_code % 8
    return (lon_source.astype(jnp.int32), lat_source.astype(jnp.int32))

def laplace(field):
    rolled = jnp.roll(field, 1, 0) + jnp.roll(field, -1, 0)
    padded = jnp.pad(field, ((0, 0), (1, 1), (0, 0)))
    return rolled + padded[:, 2:] + padded[:, :-2] - 4.0 * field

def reference(latent_state, cotangent, w_inner, w_outer, norm_gain, source_block, corner_code, frac_lon, frac_lat, terrain, kappa_table):
    lon_source, lat_source = source_cells(source_block, corner_code)
    shifts = [(0, 0), (1, 0), (0, 1), (1, 1)]
    weights = [(1.0 - frac_lon) * (1.0 - frac_lat), frac_lon * (1.0 - frac_lat), (1.0 - frac_lon) * frac_lat, frac_lon * frac_lat]
    drift = jnp.zeros((NLON, NLAT, C), jnp.float32)
    for shift, weight in zip(shifts, weights):
        picked = latent_state[lon_source + shift[0], lat_source + shift[1]].astype(jnp.float32)
        drift = drift + weight[..., None] * picked
    kappa = kappa_table[terrain][..., None]
    field = drift
    for turn_index in range(STEPS):
        field = field + kappa * laplace(field)
    flat_field = field.reshape(NLON * NLAT, C)
    rstd = lax.rsqrt(lax.optimization_barrier(jnp.mean(flat_field * flat_field, -1, keepdims=True)) + 1e-06)
    normed = flat_field * rstd
    z_in = (normed * norm_gain).astype(jnp.bfloat16)
    pre_act = jnp.dot(z_in, w_inner, preferred_element_type=jnp.float32)
    act = jax.nn.silu(pre_act).astype(jnp.bfloat16)
    react = jnp.dot(act, w_outer, preferred_element_type=jnp.float32)
    state_out = (flat_field + react).astype(jnp.bfloat16).reshape(NLON, NLAT, C)
    cot = cotangent.reshape(NLON * NLAT, C)
    grad_outer = jnp.dot(act.T, cot, preferred_element_type=jnp.float32)
    grad_act = jnp.dot(cot, w_outer.T, preferred_element_type=jnp.float32)
    sigma = jax.nn.sigmoid(pre_act)
    grad_pre = (grad_act * sigma * (1.0 + pre_act * (1.0 - sigma))).astype(jnp.bfloat16)
    grad_inner = jnp.dot(z_in.T, grad_pre, preferred_element_type=jnp.float32)
    grad_z = jnp.dot(grad_pre, w_inner.T, preferred_element_type=jnp.float32)
    grad_gain = lax.optimization_barrier(jnp.sum(grad_z * normed, 0))
    grad_norm = grad_z * norm_gain
    grad_field = cot.astype(jnp.float32) + rstd * (grad_norm - normed * lax.optimization_barrier(jnp.mean(grad_norm * normed, -1, keepdims=True)))
    grad_field = grad_field.reshape(NLON, NLAT, C)
    for turn_index in range(STEPS):
        grad_field = grad_field + laplace(kappa * grad_field)
    grad_drift = grad_field.astype(jnp.bfloat16).astype(jnp.float32)
    total = jnp.zeros((NLON, NLAT, C), jnp.float32)
    for shift, weight in zip(shifts, weights):
        part = (weight[..., None] * grad_drift).astype(jnp.bfloat16).astype(jnp.float32)
        total = total.at[lon_source + shift[0], lat_source + shift[1]].add(part)
    return (state_out, total.astype(jnp.bfloat16), grad_inner, grad_outer, grad_gain)
```

```python
import jax
import jax.numpy as jnp
from jax import lax
from jax.sharding import PartitionSpec as P

STEPS = 4
BF = jnp.bfloat16
F32 = jnp.float32


def ring_pairs(size):
    order = list(range(0, size, 2)) + list(range(size - 1, 0, -2))
    up = [(order[i], order[(i + 1) % size]) for i in range(size)]
    return up, [(j, i) for i, j in up]


def ring_place(index, size):
    return jnp.where(index % 2 == 0, index // 2, size - 1 - index // 2)


def ring_device(place, size):
    place = place % size
    return jnp.where(place < size // 2, 2 * place, 2 * (size - 1 - place) + 1)


def ring_gather(block, axis):
    size = lax.axis_size(axis)
    up, down = ring_pairs(size)
    got = [(block, 0, None)]
    a = b = block
    for s in range(1, size // 2):
        a = lax.ppermute(a, axis, up)
        b = lax.ppermute(b, axis, down)
        got += [(a, -s, None), (b, s, None)]
    half = block.shape[0] // 2
    got.append((lax.ppermute(a[:half], axis, up), size // 2, 0))
    got.append((lax.ppermute(b[half:], axis, down), size // 2, 1))
    return got


def shift_pairs(size, step, wrap):
    return [(i, (i + step) % size) for i in range(size) if wrap or 0 <= i + step < size]


def extend(value, axis, dim, width, wrap):
    size, length = lax.axis_size(axis), value.shape[dim]
    last = lax.slice_in_dim(value, length - width, length, axis=dim)
    first = lax.slice_in_dim(value, 0, width, axis=dim)
    before = lax.ppermute(last, axis, shift_pairs(size, 1, wrap))
    after = lax.ppermute(first, axis, shift_pairs(size, -1, wrap))
    return before, after


def two_point(position, start, frac):
    return jnp.where(position == start, 1.0 - frac, 0.0) + jnp.where(position == start + 1, frac, 0.0)


def halve(value, axis, bit):
    size = lax.axis_size(axis)
    index = lax.axis_index(axis)
    half = value.shape[0] // 2
    upper = (index // bit) % 2
    keep = lax.dynamic_slice_in_dim(value, upper * half, half, 0)
    send = lax.dynamic_slice_in_dim(value, (1 - upper) * half, half, 0)
    other = lax.ppermute(send, axis, [(i, i ^ bit) for i in range(size)])
    return (keep.astype(F32) + other.astype(F32)).astype(BF)


def rejoin(value, axis, bit):
    size = lax.axis_size(axis)
    upper = (lax.axis_index(axis) // bit) % 2
    other = lax.ppermute(value, axis, [(i, i ^ bit) for i in range(size)])
    return jnp.where(
        upper == 1,
        jnp.concatenate([other, value], 0),
        jnp.concatenate([value, other], 0),
    )


def bits_of(size):
    bit, found = 1, []
    while bit < size:
        found.append(bit)
        bit *= 2
    return found


def sum_all(value):
    lat_bits = bits_of(lax.axis_size("lat"))
    for bit in lat_bits:
        value = halve(value, "lat", bit)
    value = halve(value, "lon", 1)
    size = lax.axis_size("lon")
    groups = size // 2
    place = lax.axis_index("lon") // 2
    piece = value.shape[0] // groups
    total = lax.dynamic_slice_in_dim(value, place * piece, piece, 0).astype(F32)
    for k in range(1, groups):
        send = lax.dynamic_slice_in_dim(value, (place + k) % groups * piece, piece, 0)
        got = lax.ppermute(send, "lon", shift_pairs(size, 2 * k, True))
        total = total + got.astype(F32)
    own = total.astype(BF)
    parts = [own] + [
        lax.ppermute(own, "lon", shift_pairs(size, -2 * k, True)) for k in range(1, groups)
    ]
    both = jnp.concatenate(parts + parts, 0)
    value = lax.dynamic_slice_in_dim(both, (groups - place) % groups * piece, groups * piece, 0)
    value = rejoin(value, "lon", 1)
    for bit in reversed(lat_bits):
        value = rejoin(value, "lat", bit)
    return value


def sum_small(value):
    for axis in ("lat", "lon"):
        size = lax.axis_size(axis)
        for bit in bits_of(size):
            value = value + lax.ppermute(value, axis, [(i, i ^ bit) for i in range(size)])
    return value


def inner_laplace(field):
    middle = field[1:-1, 1:-1]
    return field[2:, 1:-1] + field[:-2, 1:-1] + field[1:-1, 2:] + field[1:-1, :-2] - 4.0 * middle


def on_device(
    latent_state,
    cotangent,
    w_inner,
    w_outer,
    norm_gain,
    source_block,
    corner_code,
    frac_lon,
    frac_lat,
    terrain,
    kappa_table,
):
    lon_cells, lat_cells, chans = latent_state.shape
    hid = w_inner.shape[1]
    cells = lon_cells * lat_cells
    size = lax.axis_size("lon")
    me = lax.axis_index("lon")
    place = ring_place(me, size)
    reach = 2 * STEPS
    per_row = lat_cells // 8
    lon_src = source_block // per_row * 8 + corner_code // 8
    lat_src = source_block % per_row * 8 + corner_code % 8
    classes = jnp.arange(kappa_table.shape[0], dtype=jnp.int32)
    kappa = jnp.sum(jnp.where(terrain[..., None] == classes, kappa_table, 0.0), -1)
    meta = jnp.stack([lon_src.astype(F32), lat_src.astype(F32), frac_lon, frac_lat, kappa])
    before, after = extend(meta, "lon", 1, reach, True)
    meta_wide = jnp.concatenate([before, meta, after], 1)
    kap_before, kap_after = extend(meta_wide[4], "lat", 1, reach, False)
    kappa_wide = jnp.concatenate([kap_before, meta_wide[4], kap_after], 1)[..., None]
    cot_before, cot_after = extend(cotangent, "lat", 1, STEPS, False)
    cot_tall = jnp.concatenate([cot_before, cotangent, cot_after], 1)
    cot_left, cot_right = extend(cot_tall, "lon", 0, STEPS, True)
    cot_wide = jnp.concatenate([cot_left, cot_tall, cot_right], 0)

    lon_of = jnp.arange(cells, dtype=jnp.int32) // lat_cells
    lat_of = jnp.arange(cells, dtype=jnp.int32) % lat_cells
    columns = meta_wide[:4].reshape(4, -1, 1)
    dev = columns[0].astype(jnp.int32) // lon_cells
    table = two_point(lon_of[None, :], columns[0].astype(jnp.int32) % lon_cells, columns[2])
    table = table * two_point(lat_of[None, :], columns[1].astype(jnp.int32), columns[3])
    drift = jnp.zeros((table.shape[0], chans), F32)
    half = cells // 2
    for block, offset, part in ring_gather(latent_state, "lon"):
        source = ring_device(place + offset, size)
        piece = table if part is None else table[:, part * half : (part + 1) * half]
        chosen = jnp.where(dev == source, piece, 0.0)
        upper = chosen.astype(BF)
        lower = (chosen - upper.astype(F32)).astype(BF)
        flat = block.reshape(-1, chans)
        drift = drift + jnp.dot(upper, flat, preferred_element_type=F32)
        drift = drift + jnp.dot(lower, flat, preferred_element_type=F32)
    drift = drift.reshape(-1, lat_cells, chans)
    low, high = extend(drift.astype(BF), "lat", 1, reach, False)
    field = jnp.concatenate([low.astype(F32), drift, high.astype(F32)], 1)
    kappa_run = kappa_wide
    for turn_index in range(STEPS):
        kappa_run = kappa_run[1:-1, 1:-1]
        field = field[1:-1, 1:-1] + kappa_run * inner_laplace(field)
    wide_lon, wide_lat = field.shape[:2]
    flat_field = field.reshape(-1, chans)
    rstd = lax.rsqrt(jnp.mean(flat_field * flat_field, -1, keepdims=True) + 1e-06)
    normed = flat_field * rstd
    z_in = (normed * norm_gain).astype(BF)
    pre_act = jnp.dot(z_in, w_inner, preferred_element_type=F32)
    act = jax.nn.silu(pre_act).astype(BF)

    def centre(value):
        shaped = value.reshape(wide_lon, wide_lat, value.shape[-1])
        return shaped[STEPS:-STEPS, STEPS:-STEPS].reshape(cells, value.shape[-1])

    act_mid = centre(act)
    react = jnp.dot(act_mid, w_outer, preferred_element_type=F32)
    state_out = (centre(flat_field) + react).astype(BF).reshape(lon_cells, lat_cells, chans)
    cot = cot_wide.reshape(-1, chans)
    local_outer = jnp.dot(act_mid.T, cotangent.reshape(cells, chans), preferred_element_type=F32)
    grad_act = jnp.dot(cot, w_outer.T, preferred_element_type=F32)
    sigma = jax.nn.sigmoid(pre_act)
    grad_pre = (grad_act * sigma * (1.0 + pre_act * (1.0 - sigma))).astype(BF)
    local_inner = jnp.dot(centre(z_in).T, centre(grad_pre), preferred_element_type=F32)
    grad_z = jnp.dot(grad_pre, w_inner.T, preferred_element_type=F32)
    local_gain = jnp.sum(centre(grad_z * normed), 0, keepdims=True)
    grad_norm = grad_z * norm_gain
    grad_field = cot.astype(F32) + rstd * (
        grad_norm - normed * jnp.mean(grad_norm * normed, -1, keepdims=True)
    )
    grad_field = grad_field.reshape(wide_lon, wide_lat, chans)
    for turn_index in range(STEPS):
        grad_field = grad_field[1:-1, 1:-1] + inner_laplace(kappa_run * grad_field)
        kappa_run = kappa_run[1:-1, 1:-1]
    grad_drift = grad_field.astype(BF)

    stacked = jnp.concatenate(
        [local_inner[:, : hid // 2], local_inner[:, hid // 2 :], local_outer], 0
    ).astype(BF)
    stacked = sum_all(stacked)
    grad_inner = jnp.concatenate([stacked[:chans], stacked[chans : 2 * chans]], 1).astype(F32)
    grad_outer = stacked[2 * chans :].astype(F32)
    grad_gain = sum_small(local_gain).reshape(chans)

    metas = ring_gather(meta[:4].reshape(4, 1, cells).astype(F32), "lon")
    total = jnp.zeros((cells, chans), F32)
    blocks = ring_gather(grad_drift, "lon")
    rows = {}
    for block, offset, part in metas:
        rows.setdefault(offset, []).append(block)
    for block, offset, part in blocks:
        row = jnp.concatenate(rows[offset], 0)
        if part is not None:
            row = row[..., part * half : (part + 1) * half]
        lon_row, lat_row = row[0].astype(jnp.int32), row[1].astype(jnp.int32)
        entry = two_point(lon_of[:, None], lon_row - me * lon_cells, row[2])
        entry = jnp.where(lon_row // lon_cells == me, entry, 0.0)
        entry = entry * two_point(lat_of[:, None], lat_row, row[3])
        total = total + jnp.dot(
            entry.astype(BF), block.reshape(-1, chans), preferred_element_type=F32
        )
    summed = total.astype(BF).reshape(lon_cells, lat_cells, chans)
    return (state_out, summed, grad_inner, grad_outer, grad_gain)


def solution(mesh):
    tile = P("lon", "lat", None)
    plane = P("lon", "lat")
    placed = (tile, tile, P(), P(), P(), plane, plane, plane, plane, plane, P())
    return jax.shard_map(
        on_device,
        mesh=mesh,
        in_specs=placed,
        out_specs=(tile, tile, P(), P(), P()),
        check_vma=False,
    )
```
